32 devices in a mesh: tile: 4 (over y, core), tm: 8 (over z, x).
Axes of the slice: x: 2, y: 2, z: 4, core: 2. Of those that a mesh axis runs over, the one named last changes fastest.
Arguments:
- pixels: bfloat16 [192, 16, 64, 256], P(('tile', 'tm')), may hold values from -6 to 6
- slot_tile: int32 [192], replicated, may hold values from -1 to 95, as said below
- w_space: bfloat16 [3, 3, 256, 512], replicated, may hold values from -0.125 to 0.125
- b_space: float32 [512], replicated, may hold values from -3 to 3
- w_time: bfloat16 [3, 512, 512], replicated, may hold values from -0.15625 to 0.15625
- b_time: float32 [512], replicated, may hold values from -3 to 3
- gain: float32 [512], replicated, may hold values from 0.1 to 1.9
Outputs:
- latent: bfloat16 [96, 16, 16, 512], P('tile', 'tm')
The draws below stay inside these ranges and needn't reach their ends.
Inputs may be any that keep to these rules, and one draw needn't show every extreme that they name: `slot_tile`: every tile id 0..95 stands in exactly one slot, -1 marks an empty slot. On each device (the 6 slots of one device in order) the live slots come first; the devices form aligned blocks of four consecutive devices whose live slots number 2 * 3, 3, 3 and 0 in some order. A group is 24 consecutive tile ids (tile id // 24); at most 2 slots of one device hold tiles of one group, and some device holds exactly 2 of one group.
All inputs are finite; a program needn't handle non-finite values.
Results may differ from the reference program's by a relative error of at most 0.0044.
Values may be sent and summed in bfloat16 or wider, within the bound.
A program may use at most 64 MiB of HBM per device.

```python
import jax
import jax.numpy as jnp
from jax import lax

C_IN = 256
C_OUT = 512
TILE_SIDE = 8
TILE_DEV = 3
PIX = 64
CAP = 6
SLOTS = 192
TILES = 96
GROUP_TILES = 24
FRAMES = 16
N_TILE = 4
DEVICES = 32


def draw_slot_tile(key, part):
    key_loads, key_order, key_turn = jax.random.split(key, 3)
    block_count = DEVICES // 4
    pattern = jnp.array([2, 1, 1, 0], jnp.int32) * TILE_DEV
    block_keys = jax.random.split(key_loads, block_count)
    shuffles = jax.vmap(lambda block_key: jax.random.permutation(block_key, 4))(block_keys)
    loads = pattern[shuffles].reshape(DEVICES)
    offsets = jnp.cumsum(loads) - loads
    member_order = jax.random.permutation(key_order, GROUP_TILES).astype(jnp.int32)
    turn = jax.random.randint(key_turn, (), 0, N_TILE)
    slot_pos = jnp.arange(CAP, dtype=jnp.int32)
    sequence = offsets[:, None] + slot_pos[None, :]
    sequence = jnp.minimum(sequence, TILES - 1)
    group_of = (sequence % N_TILE + turn) % N_TILE
    tile_id = group_of * GROUP_TILES + member_order[sequence // N_TILE]
    result = jnp.where(slot_pos[None, :] < loads[:, None], tile_id, -1)
    return result.reshape(SLOTS).astype(jnp.int32)


def block_scale(rng, extent, cuts, low, high):
    level = 1.0
    for dim, blocks in cuts:
        steps = jax.random.uniform(jax.random.fold_in(jax.random.fold_in(rng, 6), dim), (blocks,), jnp.float32, low / len(cuts), high / len(cuts))
        level = level * jnp.repeat(jnp.exp(steps), extent[dim] // blocks).reshape((-1,) + (1,) * (len(extent) - 1 - dim))
    return level


def normal_values(key, extent, scale, reach, pieces=(), kind=jnp.bfloat16):
    level = block_scale(key, extent, pieces, -0.22, 0.18) if pieces else 1.0
    drawn = jax.random.normal(key, extent, jnp.float32) * scale * level
    return jnp.minimum(jnp.maximum(drawn, -reach), reach).astype(kind)


def setup_inputs(seed: int = 0) -> dict:
    streams_of = jax.random.split(jax.random.key(seed), 8)
    return {
        "pixels": normal_values(streams_of[0], (SLOTS, FRAMES, PIX, C_IN), 1.0, 6.0, ((0, 32),)),
        "slot_tile": draw_slot_tile(jax.random.fold_in(streams_of[7], 71), 0),
        "w_space": normal_values(streams_of[2], (3, 3, C_IN, C_OUT), (9 * C_IN) ** -0.5, 0.125),
        "b_space": normal_values(streams_of[3], (C_OUT,), 0.5, 3.0, (), jnp.float32),
        "w_time": normal_values(streams_of[4], (3, C_OUT, C_OUT), (3 * C_OUT) ** -0.5, 0.15625),
        "b_time": normal_values(streams_of[5], (C_OUT,), 0.5, 3.0, (), jnp.float32),
        "gain": jnp.clip(1.0 + 0.18 * jax.random.normal(streams_of[6], (C_OUT,), jnp.float32), 0.1, 1.9),
    }


def conv_space(raw_tiles, w_space, b_space):
    number, frames, pix_count, channels = raw_tiles.shape
    grid = raw_tiles.reshape(number * frames, TILE_SIDE, TILE_SIDE, channels)
    padded = jnp.pad(grid, ((0, 0), (1, 1), (1, 1), (0, 0)))
    half_side = TILE_SIDE // 2
    total = jnp.zeros((number * frames * half_side * half_side, w_space.shape[-1]), jnp.float32)
    for row_tap in range(3):
        for col_tap in range(3):
            patch = padded[:, row_tap:row_tap + TILE_SIDE - 1:2, col_tap:col_tap + TILE_SIDE - 1:2, :]
            total = total + jnp.dot(patch.reshape(-1, channels), w_space[row_tap, col_tap], preferred_element_type=jnp.float32)
    active = jax.nn.silu(total + b_space.astype(jnp.float32))
    return active.astype(jnp.bfloat16).reshape(number, frames, half_side * half_side, -1)

def mix_time(extended, w_time, b_time, gain):
    number, all_frames, positions, channels = extended.shape
    frames = all_frames - 2
    total = jnp.zeros((number * frames * positions, channels), jnp.float32) + b_time.astype(jnp.float32)
    for lag in range(3):
        segment = extended[:, 2 - lag:2 - lag + frames].reshape(-1, channels)
        total = total + jnp.dot(segment, w_time[lag], preferred_element_type=jnp.float32)
    mixed = extended[:, 2:].reshape(-1, channels).astype(jnp.float32) + total
    scale = lax.rsqrt(lax.optimization_barrier(jnp.mean(mixed * mixed, axis=-1, keepdims=True)) + 1e-06)
    return (mixed * scale * gain.astype(jnp.float32)).astype(jnp.bfloat16).reshape(number, frames, positions, channels)

def reference(pixels, slot_tile, w_space, b_space, w_time, b_time, gain):
    slot_count = pixels.shape[0]
    position = jnp.where(slot_tile >= 0, slot_tile, TILES).astype(jnp.int32)
    order = jnp.zeros((TILES + 1,), jnp.int32).at[position].set(jnp.arange(slot_count, dtype=jnp.int32))[:TILES]

    def encode(slot_index):
        raw_tile = lax.dynamic_index_in_dim(pixels, slot_index, 0, keepdims=True)
        spatial = conv_space(raw_tile, w_space, b_space)
        extended = jnp.pad(spatial, ((0, 0), (2, 0), (0, 0), (0, 0)))
        return mix_time(extended, w_time, b_time, gain)[0]
    return lax.map(encode, order)
```

```python
import functools

import jax
import jax.numpy as jnp
from jax import lax
from jax.experimental import pallas as pl
from jax.experimental.pallas import tpu as pltpu
from jax.sharding import PartitionSpec as P

TILE_SIDE = 8


def conv_space(raw_tiles, w_space, b_space):
    number, frames, pix_count, channels = raw_tiles.shape
    grid = raw_tiles.reshape(number * frames, TILE_SIDE, TILE_SIDE, channels)
    total = lax.conv_general_dilated(
        grid,
        w_space,
        (2, 2),
        ((1, 1), (1, 1)),
        dimension_numbers=("NHWC", "HWIO", "NHWC"),
        preferred_element_type=jnp.float32,
    )
    active = jax.nn.silu(total + b_space)
    half_side = TILE_SIDE // 2
    return active.astype(jnp.bfloat16).reshape(number, frames, half_side * half_side, -1)


def tables(slot_tile, rows, groups, bucket, group_tiles, my_row):
    table = slot_tile.reshape(rows, -1)
    width = table.shape[1]
    group_of = jnp.where(table >= 0, lax.div(table, group_tiles), groups)
    pos = jnp.arange(width, dtype=jnp.int32)
    earlier = pos[None, :] < pos[:, None]
    same = (group_of[:, :, None] == group_of[:, None, :]) & earlier[None]
    rank = jnp.sum(same.astype(jnp.int32), axis=2)
    target = group_of * bucket + rank
    own_target = lax.dynamic_index_in_dim(target, my_row, 0, keepdims=False)
    own_live = lax.dynamic_index_in_dim(table, my_row, 0, keepdims=False) >= 0
    own_target = jnp.where(own_live, own_target, -1)
    places = jnp.arange(groups * bucket, dtype=jnp.int32)
    send_idx = jnp.sum(
        jnp.where(own_target[None, :] == places[:, None], pos[None, :], 0), axis=1
    )
    wanted = my_row * group_tiles + jnp.arange(group_tiles, dtype=jnp.int32)
    arrived = jnp.arange(rows, dtype=jnp.int32)[:, None] * bucket + rank
    pick_idx = jnp.sum(
        jnp.where(
            table.reshape(-1)[None, :] == wanted[:, None], arrived.reshape(-1)[None, :], 0
        ),
        axis=1,
    )
    return send_idx, pick_idx


def kernel(
    rows, slabs, cap, bucket, group_tiles,
    send_idx, pick_idx, src, w_time, b_time, gain, out,
    got1a, got1b, out2, got2a, got2b, feats, halo,
    send1, recv1, send2, recv2, send3, recv3,
):
    frames = 2
    got1, got2 = (got1a, got1b), (got2a, got2b)
    row = lax.axis_index("tile")
    slab = lax.axis_index("tm")
    barrier = pltpu.get_barrier_semaphore()
    for k in range(1, slabs):
        pl.semaphore_signal(barrier, inc=1, device_id={"tm": lax.rem(slab + k, slabs)})
    for k in range(1, rows):
        pl.semaphore_signal(barrier, inc=1, device_id={"tile": lax.rem(row + k, rows)})
    pl.semaphore_wait(barrier, slabs + rows - 2)

    def copy1(f, k):
        to = lax.rem(slab + k, slabs)
        return pltpu.make_async_remote_copy(
            src_ref=src.at[to, f],
            dst_ref=got1[f].at[pl.ds(slab * cap, cap)],
            send_sem=send1.at[f, k - 1],
            recv_sem=recv1.at[f, k - 1],
            device_id={"tm": to},
        )

    def copy2(f, k):
        to = lax.rem(row + k, rows)
        return pltpu.make_async_remote_copy(
            src_ref=out2.at[f, pl.ds(to * bucket, bucket)],
            dst_ref=got2[f].at[pl.ds(row * bucket, bucket)],
            send_sem=send2.at[f, k - 1],
            recv_sem=recv2.at[f, k - 1],
            device_id={"tile": to},
        )

    def copy3(f):
        return pltpu.make_async_remote_copy(
            src_ref=feats.at[f],
            dst_ref=halo.at[f],
            send_sem=send3.at[f],
            recv_sem=recv3.at[f],
            device_id={"tm": lax.rem(slab + 1, slabs)},
        )

    for f in range(frames):
        for k in range(1, slabs):
            copy1(f, k).start()
    for f in range(frames):
        got1[f][pl.ds(slab * cap, cap)] = src[slab, f]
        for k in range(1, slabs):
            copy1(f, k).wait_recv()

        @pl.loop(0, rows * bucket)
        def _(i):
            out2[f, i] = got1[f][send_idx[i]]

        for k in range(1, rows):
            copy2(f, k).start()

        @pl.loop(0, bucket)
        def _(j):
            got2[f][row * bucket + j] = got1[f][send_idx[row * bucket + j]]

        for k in range(1, rows):
            copy2(f, k).wait_recv()

        @pl.loop(0, group_tiles)
        def _(i):
            feats[f, i] = got2[f][pick_idx[i]]

        @pl.when(slab < slabs - 1)
        def _():
            copy3(f).start()

    for f in range(frames):

        @pl.when(slab > 0)
        def _():
            copy3(f).wait_recv()

        @pl.when(slab == 0)
        def _():
            halo[f] = jnp.zeros(halo.shape[1:], halo.dtype)

    part = group_tiles // 2

    @pl.loop(0, 2)
    def _(c):
        at = pl.ds(c * part, part)
        seq = [halo[0, at], halo[1, at], feats[0, at], feats[1, at]]
        seq = [v.reshape(part * 16, v.shape[-1]) for v in seq]
        for f in range(frames):
            mixed = seq[2 + f].astype(jnp.float32) + b_time[...]
            for lag in range(3):
                mixed = mixed + jnp.dot(
                    seq[2 + f - lag], w_time[lag], preferred_element_type=jnp.float32
                )
            scale = lax.rsqrt(jnp.mean(mixed * mixed, axis=-1, keepdims=True) + 1e-06)
            value = (mixed * scale * gain[...]).astype(jnp.bfloat16)
            out[at, f] = value.reshape(part, 16, value.shape[-1])

    for f in range(frames):
        for k in range(1, slabs):
            copy1(f, k).wait_send()
        for k in range(1, rows):
            copy2(f, k).wait_send()

        @pl.when(slab < slabs - 1)
        def _():
            copy3(f).wait_send()


def body(rows, slabs, pixels, slot_tile, w_space, b_space, w_time, b_time, gain):
    cap, all_frames = pixels.shape[:2]
    channels = w_space.shape[-1]
    group_tiles = cap // 2 * slabs
    per_group = (cap + rows - 1) // rows
    bucket = per_group * 3 * (slabs // 4)
    frames = all_frames // slabs
    send_idx, pick_idx = tables(
        slot_tile, rows, rows, bucket, group_tiles, lax.axis_index("tile")
    )
    spatial = conv_space(pixels, w_space, b_space)
    src = spatial.reshape(cap, slabs, frames, 16, channels).transpose(1, 2, 0, 3, 4)
    vmem = pl.BlockSpec(memory_space=pltpu.VMEM)
    smem = pl.BlockSpec(memory_space=pltpu.SMEM)
    bf16 = jnp.bfloat16
    dma = pltpu.SemaphoreType.DMA
    return pl.pallas_call(
        functools.partial(kernel, rows, slabs, cap, bucket, group_tiles),
        out_shape=jax.ShapeDtypeStruct((group_tiles, frames, 16, channels), bf16),
        in_specs=[smem, smem, vmem, vmem, vmem, vmem],
        out_specs=vmem,
        scratch_shapes=[
            pltpu.VMEM((slabs * cap, 16, channels), bf16),
            pltpu.VMEM((slabs * cap, 16, channels), bf16),
            pltpu.VMEM((frames, rows * bucket, 16, channels), bf16),
            pltpu.VMEM((rows * bucket, 16, channels), bf16),
            pltpu.VMEM((rows * bucket, 16, channels), bf16),
            pltpu.VMEM((frames, group_tiles, 16, channels), bf16),
            pltpu.VMEM((frames, group_tiles, 16, channels), bf16),
            dma((frames, slabs - 1)),
            dma((frames, slabs - 1)),
            dma((frames, rows - 1)),
            dma((frames, rows - 1)),
            dma((frames,)),
            dma((frames,)),
        ],
        compiler_params=pltpu.CompilerParams(collective_id=0, has_side_effects=True),
    )(send_idx, pick_idx, src, w_time, b_time[None], gain[None])


def solution(mesh):
    return jax.shard_map(
        functools.partial(body, mesh.shape["tile"], mesh.shape["tm"]),
        mesh=mesh,
        in_specs=(P(("tile", "tm"), None, None, None), P(), P(), P(), P(), P(), P()),
        out_specs=P("tile", "tm", None, None),
        check_vma=False,
    )
```

```python
import functools

import jax
import jax.numpy as jnp
from jax import lax
from jax.experimental import pallas as pl
from jax.experimental.pallas import tpu as pltpu
from jax.sharding import PartitionSpec as P

TILE_SIDE = 8


def conv_space(raw_tiles, w_space, b_space):
    number, frames, pix_count, channels = raw_tiles.shape
    grid = raw_tiles.reshape(number * frames, TILE_SIDE, TILE_SIDE, channels)
    total = lax.conv_general_dilated(
        grid,
        w_space,
        (2, 2),
        ((1, 1), (1, 1)),
        dimension_numbers=("NHWC", "HWIO", "NHWC"),
        preferred_element_type=jnp.float32,
    )
    active = jax.nn.silu(total + b_space)
    half_side = TILE_SIDE // 2
    return active.astype(jnp.bfloat16).reshape(number, frames, half_side * half_side, -1)


def tables(slot_tile, rows, groups, bucket, group_tiles, my_row):
    table = slot_tile.reshape(rows, -1)
    width = table.shape[1]
    group_of = jnp.where(table >= 0, lax.div(table, group_tiles), groups)
    pos = jnp.arange(width, dtype=jnp.int32)
    earlier = pos[None, :] < pos[:, None]
    same = (group_of[:, :, None] == group_of[:, None, :]) & earlier[None]
    rank = jnp.sum(same.astype(jnp.int32), axis=2)
    target = group_of * bucket + rank
    own_target = lax.dynamic_index_in_dim(target, my_row, 0, keepdims=False)
    own_live = lax.dynamic_index_in_dim(table, my_row, 0, keepdims=False) >= 0
    own_target = jnp.where(own_live, own_target, -1)
    places = jnp.arange(groups * bucket, dtype=jnp.int32)
    send_idx = jnp.sum(
        jnp.where(own_target[None, :] == places[:, None], pos[None, :], 0), axis=1
    )
    wanted = my_row * group_tiles + jnp.arange(group_tiles, dtype=jnp.int32)
    arrived = jnp.arange(rows, dtype=jnp.int32)[:, None] * bucket + rank
    pick_idx = jnp.sum(
        jnp.where(
            table.reshape(-1)[None, :] == wanted[:, None], arrived.reshape(-1)[None, :], 0
        ),
        axis=1,
    )
    return send_idx, pick_idx


def kernel(
    rows, slabs, cap, bucket, group_tiles,
    send_idx, pick_idx, src, w_time, b_time, gain, out,
    got1a, got1b, out2, got2a, got2b, feats, halo,
    send1, recv1, send2, recv2, send3, recv3,
):
    frames = 2
    got1, got2 = (got1a, got1b), (got2a, got2b)
    row = lax.axis_index("tile")
    slab = lax.axis_index("tm")
    barrier = pltpu.get_barrier_semaphore()
    for k in range(1, slabs):
        pl.semaphore_signal(barrier, inc=1, device_id={"tm": lax.rem(slab + k, slabs)})
    for k in range(1, rows):
        pl.semaphore_signal(barrier, inc=1, device_id={"tile": lax.rem(row + k, rows)})
    pl.semaphore_wait(barrier, slabs + rows - 2)

    def copy1(f, k):
        to = lax.rem(slab + k, slabs)
        return pltpu.make_async_remote_copy(
            src_ref=src.at[:, to * frames + f],
            dst_ref=got1[f].at[pl.ds(slab * cap, cap)],
            send_sem=send1.at[f, k - 1],
            recv_sem=recv1.at[f, k - 1],
            device_id={"tm": to},
        )

    def copy2(f, k):
        to = lax.rem(row + k, rows)
        return pltpu.make_async_remote_copy(
            src_ref=out2.at[f, pl.ds(to * bucket, bucket)],
            dst_ref=got2[f].at[pl.ds(row * bucket, bucket)],
            send_sem=send2.at[f, k - 1],
            recv_sem=recv2.at[f, k - 1],
            device_id={"tile": to},
        )

    def copy3(f):
        return pltpu.make_async_remote_copy(
            src_ref=feats.at[f],
            dst_ref=halo.at[f],
            send_sem=send3.at[f],
            recv_sem=recv3.at[f],
            device_id={"tm": lax.rem(slab + 1, slabs)},
        )

    for f in range(frames):
        for k in range(1, slabs):
            copy1(f, k).start()
    for f in range(frames):
        got1[f][pl.ds(slab * cap, cap)] = src[:, slab * frames + f]
        for k in range(1, slabs):
            copy1(f, k).wait_recv()

        @pl.loop(0, rows * bucket)
        def _(i):
            out2[f, i] = got1[f][send_idx[i]]

        for k in range(1, rows):
            copy2(f, k).start()

        @pl.loop(0, bucket)
        def _(j):
            got2[f][row * bucket + j] = got1[f][send_idx[row * bucket + j]]

        for k in range(1, rows):
            copy2(f, k).wait_recv()

        @pl.loop(0, group_tiles)
        def _(i):
            feats[f, i] = got2[f][pick_idx[i]]

        @pl.when(slab < slabs - 1)
        def _():
            copy3(f).start()

    for f in range(frames):

        @pl.when(slab > 0)
        def _():
            copy3(f).wait_recv()

        @pl.when(slab == 0)
        def _():
            halo[f] = jnp.zeros(halo.shape[1:], halo.dtype)

    part = group_tiles // 2

    @pl.loop(0, 2)
    def _(c):
        at = pl.ds(c * part, part)
        seq = [halo[0, at], halo[1, at], feats[0, at], feats[1, at]]
        seq = [v.reshape(part * 16, v.shape[-1]) for v in seq]
        for f in range(frames):
            mixed = seq[2 + f].astype(jnp.float32) + b_time[...]
            for lag in range(3):
                mixed = mixed + jnp.dot(
                    seq[2 + f - lag], w_time[lag], preferred_element_type=jnp.float32
                )
            scale = lax.rsqrt(jnp.mean(mixed * mixed, axis=-1, keepdims=True) + 1e-06)
            value = (mixed * scale * gain[...]).astype(jnp.bfloat16)
            out[at, f] = value.reshape(part, 16, value.shape[-1])

    for f in range(frames):
        for k in range(1, slabs):
            copy1(f, k).wait_send()
        for k in range(1, rows):
            copy2(f, k).wait_send()

        @pl.when(slab < slabs - 1)
        def _():
            copy3(f).wait_send()


def body(rows, slabs, pixels, slot_tile, w_space, b_space, w_time, b_time, gain):
    cap, all_frames = pixels.shape[:2]
    channels = w_space.shape[-1]
    group_tiles = cap // 2 * slabs
    per_group = (cap + rows - 1) // rows
    bucket = per_group * 3 * (slabs // 4)
    frames = all_frames // slabs
    send_idx, pick_idx = tables(
        slot_tile, rows, rows, bucket, group_tiles, lax.axis_index("tile")
    )
    spatial = conv_space(pixels, w_space, b_space)
    vmem = pl.BlockSpec(memory_space=pltpu.VMEM)
    smem = pl.BlockSpec(memory_space=pltpu.SMEM)
    bf16 = jnp.bfloat16
    dma = pltpu.SemaphoreType.DMA
    return pl.pallas_call(
        functools.partial(kernel, rows, slabs, cap, bucket, group_tiles),
        out_shape=jax.ShapeDtypeStruct((group_tiles, frames, 16, channels), bf16),
        in_specs=[smem, smem, vmem, vmem, vmem, vmem],
        out_specs=vmem,
        scratch_shapes=[
            pltpu.VMEM((slabs * cap, 16, channels), bf16),
            pltpu.VMEM((slabs * cap, 16, channels), bf16),
            pltpu.VMEM((frames, rows * bucket, 16, channels), bf16),
            pltpu.VMEM((rows * bucket, 16, channels), bf16),
            pltpu.VMEM((rows * bucket, 16, channels), bf16),
            pltpu.VMEM((frames, group_tiles, 16, channels), bf16),
            pltpu.VMEM((frames, group_tiles, 16, channels), bf16),
            dma((frames, slabs - 1)),
            dma((frames, slabs - 1)),
            dma((frames, rows - 1)),
            dma((frames, rows - 1)),
            dma((frames,)),
            dma((frames,)),
        ],
        compiler_params=pltpu.CompilerParams(collective_id=0, has_side_effects=True),
    )(send_idx, pick_idx, spatial, w_time, b_time[None], gain[None])


def solution(mesh):
    return jax.shard_map(
        functools.partial(body, mesh.shape["tile"], mesh.shape["tm"]),
        mesh=mesh,
        in_specs=(P(("tile", "tm"), None, None, None), P(), P(), P(), P(), P(), P()),
        out_specs=P("tile", "tm", None, None),
        check_vma=False,
    )
```

```python
import functools

import jax
import jax.numpy as jnp
from jax import lax
from jax.experimental import pallas as pl
from jax.experimental.pallas import tpu as pltpu
from jax.sharding import PartitionSpec as P

TILE_SIDE = 8


def conv_space(raw_tiles, w_space, b_space):
    number, frames, pix_count, channels = raw_tiles.shape
    grid = raw_tiles.reshape(number * frames, TILE_SIDE, TILE_SIDE, channels)
    total = lax.conv_general_dilated(
        grid,
        w_space,
        (2, 2),
        ((1, 1), (1, 1)),
        dimension_numbers=("NHWC", "HWIO", "NHWC"),
        preferred_element_type=jnp.float32,
    )
    active = jax.nn.silu(total + b_space)
    half_side = TILE_SIDE // 2
    return active.astype(jnp.bfloat16).reshape(number, frames, half_side * half_side, -1)


def tables(slot_tile, rows, groups, bucket, group_tiles, my_row):
    table = slot_tile.reshape(rows, -1)
    width = table.shape[1]
    group_of = jnp.where(table >= 0, lax.div(table, group_tiles), groups)
    pos = jnp.arange(width, dtype=jnp.int32)
    earlier = pos[None, :] < pos[:, None]
    same = (group_of[:, :, None] == group_of[:, None, :]) & earlier[None]
    rank = jnp.sum(same.astype(jnp.int32), axis=2)
    target = group_of * bucket + rank
    own_target = lax.dynamic_index_in_dim(target, my_row, 0, keepdims=False)
    own_live = lax.dynamic_index_in_dim(table, my_row, 0, keepdims=False) >= 0
    own_target = jnp.where(own_live, own_target, -1)
    places = jnp.arange(groups * bucket, dtype=jnp.int32)
    send_idx = jnp.sum(
        jnp.where(own_target[None, :] == places[:, None], pos[None, :], 0), axis=1
    )
    wanted = my_row * group_tiles + jnp.arange(group_tiles, dtype=jnp.int32)
    arrived = jnp.arange(rows, dtype=jnp.int32)[:, None] * bucket + rank
    pick_idx = jnp.sum(
        jnp.where(
            table.reshape(-1)[None, :] == wanted[:, None], arrived.reshape(-1)[None, :], 0
        ),
        axis=1,
    )
    return send_idx, pick_idx


def kernel(
    rows, slabs, cap, bucket, group_tiles,
    send_idx, pick_idx, src, w_time, b_time, gain, out,
    got1a, got1b, out2, got2a, got2b, feats, halo, total,
    send1, recv1, send2, recv2, send3, recv3,
):
    frames = 2
    got1, got2 = (got1a, got1b), (got2a, got2b)
    row = lax.axis_index("tile")
    slab = lax.axis_index("tm")
    barrier = pltpu.get_barrier_semaphore()
    for k in range(1, slabs):
        pl.semaphore_signal(barrier, inc=1, device_id={"tm": lax.rem(slab + k, slabs)})
    for k in range(1, rows):
        pl.semaphore_signal(barrier, inc=1, device_id={"tile": lax.rem(row + k, rows)})
    pl.semaphore_wait(barrier, slabs + rows - 2)

    def copy1(f, k):
        to = lax.rem(slab + k, slabs)
        return pltpu.make_async_remote_copy(
            src_ref=src.at[:, to * frames + f],
            dst_ref=got1[f].at[pl.ds(slab * cap, cap)],
            send_sem=send1.at[f, k - 1],
            recv_sem=recv1.at[f, k - 1],
            device_id={"tm": to},
        )

    def copy2(f, k):
        to = lax.rem(row + k, rows)
        return pltpu.make_async_remote_copy(
            src_ref=out2.at[f, pl.ds(to * bucket, bucket)],
            dst_ref=got2[f].at[pl.ds(row * bucket, bucket)],
            send_sem=send2.at[f, k - 1],
            recv_sem=recv2.at[f, k - 1],
            device_id={"tile": to},
        )

    def copy3(f):
        return pltpu.make_async_remote_copy(
            src_ref=feats.at[f],
            dst_ref=halo.at[f],
            send_sem=send3.at[f],
            recv_sem=recv3.at[f],
            device_id={"tm": lax.rem(slab + 1, slabs)},
        )

    for f in range(frames):
        for k in range(1, slabs):
            copy1(f, k).start()
    for f in range(frames):
        got1[f][pl.ds(slab * cap, cap)] = src[:, slab * frames + f]
        for k in range(1, slabs):
            copy1(f, k).wait_recv()

        @pl.loop(0, rows * bucket)
        def _(i):
            out2[f, i] = got1[f][send_idx[i]]

        for k in range(1, rows):
            copy2(f, k).start()

        @pl.loop(0, bucket)
        def _(j):
            got2[f][row * bucket + j] = got1[f][send_idx[row * bucket + j]]

        for k in range(1, rows):
            copy2(f, k).wait_recv()

        @pl.loop(0, group_tiles)
        def _(i):
            feats[f, i] = got2[f][pick_idx[i]]

        @pl.when(slab < slabs - 1)
        def _():
            copy3(f).start()

    part = group_tiles // 2
    height = part * 16

    def flat(value):
        return value.reshape(height, value.shape[-1])

    @pl.loop(0, 2)
    def _(c):
        at = pl.ds(c * part, part)
        own = [flat(feats[0, at]), flat(feats[1, at])]
        for f in range(frames):
            mixed = own[f].astype(jnp.float32) + b_time[...]
            for lag in range(f + 1):
                mixed = mixed + jnp.dot(
                    own[f - lag], w_time[lag], preferred_element_type=jnp.float32
                )
            total[f, c] = mixed

    for f in range(frames):

        @pl.when(slab > 0)
        def _():
            copy3(f).wait_recv()

        @pl.when(slab == 0)
        def _():
            halo[f] = jnp.zeros(halo.shape[1:], halo.dtype)

    @pl.loop(0, 2)
    def _(c):
        at = pl.ds(c * part, part)
        before = [flat(halo[0, at]), flat(halo[1, at])]
        for f in range(frames):
            mixed = total[f, c]
            for lag in range(f + 1, 3):
                mixed = mixed + jnp.dot(
                    before[2 + f - lag], w_time[lag], preferred_element_type=jnp.float32
                )
            scale = lax.rsqrt(jnp.mean(mixed * mixed, axis=-1, keepdims=True) + 1e-06)
            value = (mixed * scale * gain[...]).astype(jnp.bfloat16)
            out[at, f] = value.reshape(part, 16, value.shape[-1])

    for f in range(frames):
        for k in range(1, slabs):
            copy1(f, k).wait_send()
        for k in range(1, rows):
            copy2(f, k).wait_send()

        @pl.when(slab < slabs - 1)
        def _():
            copy3(f).wait_send()


def body(rows, slabs, pixels, slot_tile, w_space, b_space, w_time, b_time, gain):
    cap, all_frames = pixels.shape[:2]
    channels = w_space.shape[-1]
    group_tiles = cap // 2 * slabs
    per_group = (cap + rows - 1) // rows
    bucket = per_group * 3 * (slabs // 4)
    frames = all_frames // slabs
    send_idx, pick_idx = tables(
        slot_tile, rows, rows, bucket, group_tiles, lax.axis_index("tile")
    )
    spatial = conv_space(pixels, w_space, b_space)
    vmem = pl.BlockSpec(memory_space=pltpu.VMEM)
    smem = pl.BlockSpec(memory_space=pltpu.SMEM)
    bf16 = jnp.bfloat16
    dma = pltpu.SemaphoreType.DMA
    return pl.pallas_call(
        functools.partial(kernel, rows, slabs, cap, bucket, group_tiles),
        out_shape=jax.ShapeDtypeStruct((group_tiles, frames, 16, channels), bf16),
        in_specs=[smem, smem, vmem, vmem, vmem, vmem],
        out_specs=vmem,
        scratch_shapes=[
            pltpu.VMEM((slabs * cap, 16, channels), bf16),
            pltpu.VMEM((slabs * cap, 16, channels), bf16),
            pltpu.VMEM((frames, rows * bucket, 16, channels), bf16),
            pltpu.VMEM((rows * bucket, 16, channels), bf16),
            pltpu.VMEM((rows * bucket, 16, channels), bf16),
            pltpu.VMEM((frames, group_tiles, 16, channels), bf16),
            pltpu.VMEM((frames, group_tiles, 16, channels), bf16),
            pltpu.VMEM((frames, 2, group_tiles * 8, channels), jnp.float32),
            dma((frames, slabs - 1)),
            dma((frames, slabs - 1)),
            dma((frames, rows - 1)),
            dma((frames, rows - 1)),
            dma((frames,)),
            dma((frames,)),
        ],
        compiler_params=pltpu.CompilerParams(collective_id=0, has_side_effects=True),
    )(send_idx, pick_idx, spatial, w_time, b_time[None], gain[None])


def solution(mesh):
    return jax.shard_map(
        functools.partial(body, mesh.shape["tile"], mesh.shape["tm"]),
        mesh=mesh,
        in_specs=(P(("tile", "tm"), None, None, None), P(), P(), P(), P(), P(), P()),
        out_specs=P("tile", "tm", None, None),
        check_vma=False,
    )
```
